32 devices in a mesh: mp: 8 (over z, x), head: 4 (over y, core).
Axes of the slice: x: 2, y: 2, z: 4, core: 2. Of those that a mesh axis runs over, the one named last changes fastest.
Arguments:
- hidden: bfloat16 [8, 4096], replicated, may hold values from -6 to 6
- norm_gain: float32 [4096], replicated, may hold values from 0.25 to 1.75
- w_query: bfloat16 [4096, 4096], P('mp', 'head'), may hold values from -0.09375 to 0.09375
- enc_states: bfloat16 [8, 512, 4096], P(None, 'mp'), may hold values from -6 to 6
- w_key: bfloat16 [4096, 4096], P('mp', 'head'), may hold values from -0.09375 to 0.09375
- w_value: bfloat16 [4096, 4096], P('mp', 'head'), may hold values from -0.09375 to 0.09375
- w_out: bfloat16 [4096, 4096], P('head', 'mp'), may hold values from -0.09375 to 0.09375
- bias_table: float32 [32, 64], P(None, 'head'), may hold values from -5 to 300
- buckets: int32 [8, 512], P(None, 'mp'), may hold values from 0 to 31
- src_len: int32 [8], replicated, may hold values from 64 to 512
Outputs:
- updated: bfloat16 [8, 4096], P(None, 'mp')
The draws below stay inside these ranges and needn't reach their ends.
All inputs are finite; a program needn't handle non-finite values.
Results may differ from the reference program's by a relative error of at most 0.0049.
Values may be sent and summed in bfloat16 or wider, within the bound.
No kernel may reach another device: no remote copies, remote signals or barrier semaphores. Data moves between devices by JAX's collectives and lax.ppermute only.
A program may use at most 128 MiB of HBM per device.

```python
import jax
import jax.numpy as jnp
from jax import lax

D = 4096
HEADS = 64
DH = 64
BUCKETS = 32
BATCH = 8
INNER = 4096
S = 512


def draw_bias_table(key, part):
    base_key = jax.random.fold_in(jax.random.fold_in(key, 7), 0)
    result = jnp.clip(jax.random.normal(base_key, (BUCKETS, HEADS), jnp.float32), -5.0, 5.0)
    return result


def place_ends(drawn, rng, smallest, largest):
    spot = [jax.random.randint(jax.random.fold_in(rng, axis), (), 0, length) for axis, length in enumerate(drawn.shape)]
    longest = drawn.shape.index(max(drawn.shape))
    next_to = spot[:longest] + [(spot[longest] + 1) % drawn.shape[longest]] + spot[longest + 1:]
    return drawn.at[tuple(spot)].set(smallest).at[tuple(next_to)].set(largest)


def shard_levels(own_key, dims, cuts, least, largest):
    gain, own = 1.0, jax.random.fold_in(own_key, 6)
    for dim, shards_of in cuts:
        heights = jnp.exp(jax.random.uniform(jax.random.fold_in(own, dim), (shards_of,), jnp.float32, least / len(cuts), largest / len(cuts)))
        gain = gain * jnp.repeat(heights, dims[dim] // shards_of).reshape([-1 if axis == dim else 1 for axis in range(len(dims))])
    return gain


def centred(key, shape, width, most, pieces=(), kind=jnp.bfloat16):
    entries = width * jax.random.normal(key, shape, jnp.float32)
    if pieces:
        entries = entries * shard_levels(key, shape, pieces, -0.22, 0.18)
    return jnp.clip(entries, -most, most).astype(kind)


def setup_inputs(seed: int = 0) -> dict:
    splits = jax.random.split(jax.random.key(seed), 11)
    return {
        "hidden": centred(splits[0], (BATCH, D), 1.0, 6.0),
        "norm_gain": jnp.clip(1.0 + 0.15 * jax.random.normal(splits[1], (D,), jnp.float32), 0.25, 1.75),
        "w_query": centred(splits[2], (D, INNER), D ** -0.5, 0.09375, ((0, 8), (1, 4))),
        "enc_states": centred(splits[3], (BATCH, S, D), 1.0, 6.0, ((1, 8),)),
        "w_key": centred(splits[4], (D, INNER), D ** -0.5, 0.09375, ((0, 8), (1, 4))),
        "w_value": centred(splits[5], (D, INNER), D ** -0.5, 0.09375, ((0, 8), (1, 4))),
        "w_out": centred(splits[6], (INNER, D), INNER ** -0.5, 0.09375, ((0, 4), (1, 8))),
        "bias_table": draw_bias_table(jax.random.fold_in(splits[10], 71), 0),
        "buckets": place_ends(jax.random.randint(splits[8], (BATCH, S), 0, BUCKETS), jax.random.fold_in(splits[8], 1), 0, BUCKETS - 1).astype(jnp.int32),
        "src_len": place_ends(jax.random.randint(splits[9], (BATCH,), S // 8, S + 1), jax.random.fold_in(splits[9], 1), S // 8, S).astype(jnp.int32),
    }


EPSILON = 1e-06
NEGATIVE = -1e+30

def reference(hidden, norm_gain, w_query, enc_states, w_key, w_value, w_out, bias_table, buckets, src_len):
    widened = hidden.astype(jnp.float32)
    mean_square = lax.optimization_barrier(jnp.mean(widened * widened, axis=-1, keepdims=True))
    normed = (widened * lax.rsqrt(mean_square + EPSILON) * norm_gain.astype(jnp.float32)).astype(jnp.bfloat16)
    query = jnp.dot(normed, w_query, preferred_element_type=jnp.float32).astype(jnp.bfloat16)
    query = query.reshape(BATCH, HEADS, DH)
    flat_rows = enc_states.reshape(BATCH * S, D)
    key_rows = jnp.dot(flat_rows, w_key, preferred_element_type=jnp.float32)
    value_rows = jnp.dot(flat_rows, w_value, preferred_element_type=jnp.float32)
    key_rows = key_rows.reshape(BATCH, S, HEADS, DH)
    value_rows = value_rows.reshape(BATCH, S, HEADS, DH)
    factor = float(DH) ** (-0.5)
    scores = jnp.einsum('bhd,bshd->bhs', query.astype(jnp.float32), key_rows, precision=lax.Precision.HIGHEST) * factor
    scores = scores + jnp.transpose(bias_table[buckets], (0, 2, 1))
    is_live = (jnp.arange(S, dtype=jnp.int32)[None, :] < src_len[:, None])[:, None, :]
    scores = jnp.where(is_live, scores, NEGATIVE)
    best_max = lax.optimization_barrier(jnp.max(scores, axis=-1, keepdims=True))
    weights = jnp.where(is_live, jnp.exp(scores - best_max), 0.0)
    denominator = lax.optimization_barrier(jnp.sum(weights, axis=-1))
    weighted = jnp.einsum('bhs,bshd->bhd', weights, value_rows, precision=lax.Precision.HIGHEST)
    context = (weighted / denominator[:, :, None]).reshape(BATCH, INNER).astype(jnp.bfloat16)
    projected = jnp.dot(context, w_out, preferred_element_type=jnp.float32)
    return (projected + widened).astype(jnp.bfloat16)
```

```python
import functools

import jax
import jax.numpy as jnp
from jax import lax
from jax.experimental import pallas as pl
from jax.experimental.pallas import tpu as pltpu
from jax.sharding import PartitionSpec as P

EPSILON = 1e-06
NEGATIVE = -1e30
ONE_SHOT = 8
EXTRA_ROWS = 16
LANES = 128


VMEM = pl.BlockSpec(memory_space=pltpu.VMEM)
SMEM = pl.BlockSpec(memory_space=pltpu.SMEM)
F32 = jnp.float32
BF16 = jnp.bfloat16


def exchange(value, axis, size, stride):
    return lax.ppermute(value, axis, [(i, i ^ stride) for i in range(size)])


def all_sum(value, axis, size):
    if size & (size - 1):
        return lax.psum(value, axis)
    stride = 1
    while stride < size:
        value = value + exchange(value, axis, size, stride)
        stride *= 2
    return value


def head_sum(value, axis, size):
    if size & (size - 1) or size > ONE_SHOT:
        return all_sum(value, axis, size)
    parts = [value] + [exchange(value, axis, size, k) for k in range(1, size)]
    while len(parts) > 1:
        parts = [sum(parts[i : i + 2]) for i in range(0, len(parts), 2)]
    return parts[0]


def dot(left, right, contract=((1,), (0,)), **kwargs):
    return lax.dot_general(left, right, (contract, ((), ())), preferred_element_type=F32, **kwargs)


def query_kernel(index_ref, hidden_ref, cols_ref, gain_ref, wq_ref, out_ref):
    panel_rows = wq_ref.shape[0]
    widened = hidden_ref[...].astype(F32)
    mean_square = jnp.mean(widened * widened, axis=-1, keepdims=True)
    window = slice(None)
    if cols_ref.shape[1] != panel_rows:
        window = pl.ds(pl.multiple_of(index_ref[0] * panel_rows, panel_rows), panel_rows)
    own = cols_ref[:, window].astype(F32) * lax.rsqrt(mean_square + EPSILON) * gain_ref[:, window]
    out_ref[...] = dot(own.astype(BF16), wq_ref[...])


def key_kernel(heads, query_ref, wk_ref, out_ref):
    batch, inner = query_ref.shape
    head_size = inner // heads
    rows = batch * heads
    query = query_ref[...].astype(BF16)
    spread = lax.broadcasted_iota(jnp.int32, (batch, rows), 1) // heads
    spread = (spread == lax.broadcasted_iota(jnp.int32, (batch, rows), 0)).astype(BF16)
    blocks = dot(query, spread, ((0,), (0,)))
    own_head = lax.broadcasted_iota(jnp.int32, (inner, rows), 0) // head_size
    row_head = lax.broadcasted_iota(jnp.int32, (inner, rows), 1) % heads
    blocks = jnp.where(own_head == row_head, blocks, 0.0).astype(BF16)
    out_ref[...] = dot(wk_ref[...], blocks).astype(BF16)


def attend_kernel(
    layout, heads, factor, index_ref, ids_ref, len_ref, enc_ref, table_ref, buckets_ref, *refs
):
    piece_refs, out_refs = refs[: len(layout)], refs[len(layout) :]
    batch, src_local = buckets_ref.shape
    kinds = table_ref.shape[0]
    rows = batch * heads
    panel_rows = piece_refs[0].shape[1]

    def window(slot):
        if len(layout) == 1:
            return slice(slot * panel_rows, (slot + 1) * panel_rows)
        return pl.ds(pl.multiple_of(ids_ref[slot] * panel_rows, panel_rows), panel_rows)

    scores = jnp.zeros((batch * src_local, rows), F32)
    slot = 0
    for ref, count in zip(piece_refs, layout):
        for i in range(count):
            scores = scores + dot(enc_ref[:, window(slot)], ref[i])
            slot += 1
    scores = scores * factor
    table = jnp.concatenate([table_ref[...]] * batch, axis=1)
    kind_ids = lax.broadcasted_iota(jnp.int32, (kinds, src_local), 0)
    bias = jnp.concatenate(
        [
            dot(
                (buckets_ref[b : b + 1, :] == kind_ids).astype(F32),
                table,
                ((0,), (0,)),
                precision=lax.Precision.HIGHEST,
            )
            for b in range(batch)
        ],
        axis=0,
    )
    position = index_ref[0] * src_local + lax.broadcasted_iota(jnp.int32, (src_local, rows), 0)
    row_batch = lax.broadcasted_iota(jnp.int32, (src_local, rows), 1) // heads
    is_live = jnp.concatenate(
        [(position < len_ref[b]) & (row_batch == b) for b in range(batch)], axis=0
    )
    scores = jnp.where(is_live, scores + bias, NEGATIVE)
    shift = jnp.max(scores, axis=0, keepdims=True).astype(BF16).astype(F32)
    weights = jnp.where(is_live, jnp.exp(scores - shift), 0.0)
    rounded = weights.astype(BF16)
    total = jnp.sum(rounded.astype(F32), axis=0, keepdims=True)
    total_high = total.astype(BF16).astype(F32)
    span = min(rows, panel_rows)
    lines = [
        scalar[:, start : start + span]
        for scalar in (shift, total_high, total - total_high)
        for start in range(0, rows, span)
    ]
    lines.append(jnp.zeros((EXTRA_ROWS - len(lines), span), F32))
    extra = jnp.concatenate(lines, axis=0).astype(BF16)
    turned = weights.T.astype(BF16)
    slot = 0
    for ref, count in zip(out_refs, layout):
        for i in range(count):
            ref[i, :rows, :] = dot(turned, enc_ref[:, window(slot)]).astype(BF16)
            ref[i, rows:, :] = jnp.zeros((EXTRA_ROWS, panel_rows), BF16)
            ref[i, rows:, :span] = extra
            slot += 1


def value_kernel(layout, heads, wv_ref, *refs):
    piece_refs, out_ref = refs[:-1], refs[-1]
    panel_rows, inner = wv_ref.shape
    rows = piece_refs[0].shape[1] - EXTRA_ROWS
    batch = rows // heads
    slots = [(ref, i) for ref, count in zip(piece_refs, layout) for i in range(count)]
    span = min(rows, panel_rows)
    count = rows // span

    def scalar(extra, which):
        lines = [extra[which * count + j : which * count + j + 1] for j in range(count)]
        return jnp.concatenate(lines, axis=1)

    extras = [ref[i, rows:, :span].astype(F32) for ref, i in slots]
    shifts = jnp.concatenate([scalar(extra, 0) for extra in extras], axis=0)
    totals = jnp.concatenate([scalar(extra, 1) + scalar(extra, 2) for extra in extras], axis=0)
    scale = jnp.exp(shifts - jnp.max(shifts, axis=0, keepdims=True))
    scale = scale / jnp.sum(scale * totals, axis=0, keepdims=True)
    scale = scale.T
    mixed = jnp.zeros((rows, panel_rows), F32)
    for slot, (ref, i) in enumerate(slots):
        mixed = mixed + scale[:, slot : slot + 1] * ref[i, :rows, :].astype(F32)
    high = mixed.astype(BF16)
    low = (mixed - high.astype(F32)).astype(BF16)
    product = dot(high, wv_ref[...]) + dot(low, wv_ref[...])
    row_head = lax.broadcasted_iota(jnp.int32, (rows, inner), 0) % heads
    own_head = lax.broadcasted_iota(jnp.int32, (rows, inner), 1) // (inner // heads)
    product = jnp.where(row_head == own_head, product, 0.0)
    out_ref[...] = jnp.sum(product.reshape(batch, heads, inner), axis=1)


def out_kernel(context_ref, wo_ref, out_ref):
    out_ref[...] = dot(context_ref[...].astype(BF16), wo_ref[...])


def call(kernel, outs, kinds):
    return pl.pallas_call(kernel, out_shape=outs, in_specs=kinds)


def shards(
    mp, head,
    hidden, norm_gain, w_query, enc_states, w_key, w_value, w_out, bias_table, buckets, src_len,
):
    batch, src_local, width = enc_states.shape
    panel_rows, inner = w_key.shape
    heads = bias_table.shape[1]
    head_size = inner // heads
    rows = batch * heads
    me = lax.axis_index("mp").astype(jnp.int32)
    index = me.reshape(1)
    aligned = panel_rows % LANES == 0
    one_shot = aligned and mp <= ONE_SHOT and mp & (mp - 1) == 0
    layout = (1,) * mp if one_shot else (mp,)
    slots = jnp.arange(mp, dtype=jnp.int32)
    ids = (slots ^ me) if one_shot else slots

    cols, gain = hidden, norm_gain.reshape(1, width)
    if not aligned:
        cols = lax.dynamic_slice_in_dim(cols, me * panel_rows, panel_rows, 1)
        gain = lax.dynamic_slice_in_dim(gain, me * panel_rows, panel_rows, 1)
    partial = call(query_kernel, jax.ShapeDtypeStruct((batch, inner), F32), [SMEM] + [VMEM] * 4)(
        index, hidden, cols, gain, w_query
    )
    query = all_sum(partial, "mp", mp)
    keyed = call(
        functools.partial(key_kernel, heads),
        jax.ShapeDtypeStruct((panel_rows, rows), BF16),
        [VMEM, VMEM],
    )(query, w_key)
    if one_shot:
        pieces = [keyed] + [exchange(keyed, "mp", mp, k) for k in range(1, mp)]
        pieces = [piece[None] for piece in pieces]
    else:
        pieces = [lax.all_gather(keyed, "mp", axis=0)]
    out_piece = [
        jax.ShapeDtypeStruct((count, rows + EXTRA_ROWS, panel_rows), BF16) for count in layout
    ]
    mixed = call(
        functools.partial(attend_kernel, layout, heads, float(head_size) ** (-0.5)),
        out_piece,
        [SMEM] * 3 + [VMEM] * (3 + len(layout)),
    )(
        index, ids, src_len, enc_states.reshape(batch * src_local, width), bias_table, buckets, *pieces
    )
    if one_shot:
        mixed = [mixed[0]] + [exchange(mixed[k], "mp", mp, k) for k in range(1, mp)]
    else:
        mixed = [lax.all_to_all(mixed[0], "mp", 0, 0, tiled=True)]
    partial = call(
        functools.partial(value_kernel, layout, heads),
        jax.ShapeDtypeStruct((batch, inner), F32),
        [VMEM] * (1 + len(layout)),
    )(w_value, *mixed)
    context = all_sum(partial, "mp", mp)
    out_cols = w_out.shape[1]
    partial = call(out_kernel, jax.ShapeDtypeStruct((batch, out_cols), F32), [VMEM, VMEM])(
        context, w_out
    )
    summed = head_sum(partial, "head", head)
    residual = lax.dynamic_slice_in_dim(hidden, me * out_cols, out_cols, 1)
    return (summed + residual.astype(F32)).astype(BF16)


def solution(mesh):
    return jax.shard_map(
        functools.partial(shards, mesh.shape["mp"], mesh.shape["head"]),
        mesh=mesh,
        in_specs=(
            P(),
            P(),
            P("mp", "head"),
            P(None, "mp", None),
            P("mp", "head"),
            P("mp", "head"),
            P("head", "mp"),
            P(None, "head"),
            P(None, "mp"),
            P(),
        ),
        out_specs=P(None, "mp"),
        check_vma=False,
    )
```

```python
import functools

import jax
import jax.numpy as jnp
from jax import lax
from jax.experimental import pallas as pl
from jax.experimental.pallas import tpu as pltpu
from jax.sharding import PartitionSpec as P

EPSILON = 1e-06
NEGATIVE = -1e30
ONE_SHOT = 8
EXTRA_ROWS = 16
LANES = 128


VMEM = pl.BlockSpec(memory_space=pltpu.VMEM)
SMEM = pl.BlockSpec(memory_space=pltpu.SMEM)
F32 = jnp.float32
BF16 = jnp.bfloat16


def exchange(value, axis, size, stride):
    return lax.ppermute(value, axis, [(i, i ^ stride) for i in range(size)])


def all_sum(value, axis, size):
    if size & (size - 1):
        return lax.psum(value, axis)
    stride = 1
    while stride < size:
        value = value + exchange(value, axis, size, stride)
        stride *= 2
    return value


def head_sum(value, axis, size):
    if size & (size - 1) or size > ONE_SHOT:
        return all_sum(value, axis, size)
    parts = [value] + [exchange(value, axis, size, k) for k in range(1, size)]
    while len(parts) > 1:
        parts = [sum(parts[i : i + 2]) for i in range(0, len(parts), 2)]
    return parts[0]


def dot(left, right, contract=((1,), (0,)), **kwargs):
    return lax.dot_general(left, right, (contract, ((), ())), preferred_element_type=F32, **kwargs)


def query_kernel(index_ref, hidden_ref, cols_ref, gain_ref, wq_ref, out_ref):
    panel_rows = wq_ref.shape[0]
    widened = hidden_ref[...].astype(F32)
    mean_square = jnp.mean(widened * widened, axis=-1, keepdims=True)
    window = slice(None)
    if cols_ref.shape[1] != panel_rows:
        window = pl.ds(pl.multiple_of(index_ref[0] * panel_rows, panel_rows), panel_rows)
    own = cols_ref[:, window].astype(F32) * lax.rsqrt(mean_square + EPSILON) * gain_ref[:, window]
    spread(out_ref, dot(own.astype(BF16), wq_ref[...]))


def key_kernel(heads, query_ref, wk_ref, out_ref):
    batch, inner = query_ref.shape[1:]
    head_size = inner // heads
    rows = batch * heads
    query = jnp.sum(query_ref[...], axis=0).astype(BF16)
    column = lax.broadcasted_iota(jnp.int32, (batch, rows), 1) // heads
    column = (column == lax.broadcasted_iota(jnp.int32, (batch, rows), 0)).astype(BF16)
    blocks = dot(query, column, ((0,), (0,)))
    own_head = lax.broadcasted_iota(jnp.int32, (inner, rows), 0) // head_size
    row_head = lax.broadcasted_iota(jnp.int32, (inner, rows), 1) % heads
    blocks = jnp.where(own_head == row_head, blocks, 0.0).astype(BF16)
    out_ref[...] = dot(wk_ref[...], blocks).astype(BF16)


def window(layout, ids_ref, slot, panel_rows):
    if layout[0] > 1:
        return slice(slot * panel_rows, (slot + 1) * panel_rows)
    return pl.ds(pl.multiple_of(ids_ref[slot] * panel_rows, panel_rows), panel_rows)


def slots_of(layout, refs):
    return [(ref, i) for ref, count in zip(refs, layout) for i in range(count)]


def score_sum(layout, ids_ref, enc_ref, refs):
    scores = None
    for slot, (ref, i) in enumerate(slots_of(layout, refs)):
        term = dot(enc_ref[:, window(layout, ids_ref, slot, ref.shape[1])], ref[i])
        scores = term if scores is None else scores + term
    return scores


def score_kernel(layout, ids_ref, enc_ref, *refs):
    refs[-1][...] = score_sum(layout, ids_ref, enc_ref, refs[:-1])


def mix_pieces(layout, ids_ref, enc_ref, turned, extra, refs):
    rows, span = turned.shape[0], extra.shape[1]
    for slot, (ref, i) in enumerate(slots_of(layout, refs)):
        panel_rows = ref.shape[2]
        ref[i, :rows, :] = dot(
            turned, enc_ref[:, window(layout, ids_ref, slot, panel_rows)]
        ).astype(BF16)
        if span != panel_rows:
            ref[i, rows:, :] = jnp.zeros((EXTRA_ROWS, panel_rows), BF16)
        ref[i, rows:, :span] = extra


def attend_kernel(
    layout, out_layout, panel_rows, heads, factor, has_part,
    index_ref, ids_ref, out_ids_ref, len_ref, enc_ref, table_ref, buckets_ref, *refs
):
    count = len(layout)
    piece_refs, refs = refs[:count], refs[count:]
    scores = score_sum(layout, ids_ref, enc_ref, piece_refs)
    if has_part:
        scores, refs = scores + refs[0][...], refs[1:]
    turned_ref, extra_ref, out_refs = refs[0], refs[1], refs[2:]
    batch, src_local = buckets_ref.shape
    kinds = table_ref.shape[0]
    rows = batch * heads
    scores = scores * factor
    table = jnp.concatenate([table_ref[...]] * batch, axis=1)
    kind_ids = lax.broadcasted_iota(jnp.int32, (kinds, src_local), 0)
    bias = jnp.concatenate(
        [
            dot(
                (buckets_ref[b : b + 1, :] == kind_ids).astype(F32),
                table,
                ((0,), (0,)),
                precision=lax.Precision.HIGHEST,
            )
            for b in range(batch)
        ],
        axis=0,
    )
    position = index_ref[0] * src_local + lax.broadcasted_iota(jnp.int32, (src_local, rows), 0)
    row_batch = lax.broadcasted_iota(jnp.int32, (src_local, rows), 1) // heads
    is_live = jnp.concatenate(
        [(position < len_ref[b]) & (row_batch == b) for b in range(batch)], axis=0
    )
    scores = jnp.where(is_live, scores + bias, NEGATIVE)
    shift = jnp.max(scores, axis=0, keepdims=True).astype(BF16).astype(F32)
    weights = jnp.where(is_live, jnp.exp(scores - shift), 0.0).astype(BF16).astype(F32)
    total = jnp.sum(weights, axis=0, keepdims=True)
    extra = extra_lines(shift, total, extra_ref.shape[1])
    extra_ref[...] = extra
    turned = weights.T.astype(BF16)
    turned_ref[...] = turned
    mix_pieces(out_layout, out_ids_ref, enc_ref, turned, extra, out_refs)


def mix_kernel(layout, ids_ref, enc_ref, turned_ref, extra_ref, *refs):
    mix_pieces(layout, ids_ref, enc_ref, turned_ref[...], extra_ref[...], refs)


def extra_lines(shift, total, span):
    high = total.astype(BF16).astype(F32)
    lines = [
        scalar[:, start : start + span]
        for scalar in (shift, high, total - high)
        for start in range(0, shift.shape[1], span)
    ]
    lines.append(jnp.zeros((EXTRA_ROWS - len(lines), span), F32))
    return jnp.concatenate(lines, axis=0).astype(BF16)


def read_extra(slots, rows, span):
    count = rows // span

    def scalar(extra, which):
        lines = [extra[which * count + j : which * count + j + 1] for j in range(count)]
        return jnp.concatenate(lines, axis=1)

    extras = [ref[i, rows:, :span].astype(F32) for ref, i in slots]
    shifts = jnp.concatenate([scalar(extra, 0) for extra in extras], axis=0)
    totals = jnp.concatenate([scalar(extra, 1) + scalar(extra, 2) for extra in extras], axis=0)
    return shifts, totals


def mix_sum(slots, scale, rows):
    scale = scale.T
    mixed = None
    for slot, (ref, i) in enumerate(slots):
        term = scale[:, slot : slot + 1] * ref[i, :rows, :].astype(F32)
        mixed = term if mixed is None else mixed + term
    return mixed


def merge_kernel(left_ref, right_ref, out_ref):
    rows, panel_rows = out_ref.shape[1] - EXTRA_ROWS, out_ref.shape[2]
    span = min(rows, panel_rows)
    slots = [(left_ref, 0), (right_ref, 0)]
    shifts, totals = read_extra(slots, rows, span)
    shift = jnp.max(shifts, axis=0, keepdims=True)
    scale = jnp.exp(shifts - shift)
    total = jnp.sum(scale * totals, axis=0, keepdims=True)
    out_ref[0, :rows, :] = mix_sum(slots, scale, rows).astype(BF16)
    if span != panel_rows:
        out_ref[0, rows:, :] = jnp.zeros((EXTRA_ROWS, panel_rows), BF16)
    out_ref[0, rows:, :span] = extra_lines(shift, total, span)


def value_kernel(layout, heads, wv_ref, *refs):
    piece_refs, out_ref = refs[:-1], refs[-1]
    panel_rows, inner = wv_ref.shape
    rows = piece_refs[0].shape[1] - EXTRA_ROWS
    batch = rows // heads
    slots = slots_of(layout, piece_refs)
    shifts, totals = read_extra(slots, rows, min(rows, panel_rows))
    scale = jnp.exp(shifts - jnp.max(shifts, axis=0, keepdims=True))
    scale = scale / jnp.sum(scale * totals, axis=0, keepdims=True)
    mixed = mix_sum(slots, scale, rows)
    high = mixed.astype(BF16)
    low = (mixed - high.astype(F32)).astype(BF16)
    product = dot(high, wv_ref[...]) + dot(low, wv_ref[...])
    row_head = lax.broadcasted_iota(jnp.int32, (rows, inner), 0) % heads
    own_head = lax.broadcasted_iota(jnp.int32, (rows, inner), 1) // (inner // heads)
    product = jnp.where(row_head == own_head, product, 0.0)
    spread(out_ref, jnp.sum(product.reshape(batch, heads, inner), axis=1))


def spread(out_ref, value):
    for i in range(out_ref.shape[0]):
        out_ref[i] = value


def out_kernel(context_ref, wo_ref, out_ref):
    out_ref[...] = dot(jnp.sum(context_ref[...], axis=0).astype(BF16), wo_ref[...])


def call(kernel, outs, scalars, arrays, limit=8):
    return pl.pallas_call(
        kernel,
        out_shape=outs,
        in_specs=[SMEM] * scalars + [VMEM] * arrays,
        compiler_params=pltpu.CompilerParams(vmem_limit_bytes=limit << 20),
    )


def shards(
    mp, head,
    hidden, norm_gain, w_query, enc_states, w_key, w_value, w_out, bias_table, buckets, src_len,
):
    batch, src_local, width = enc_states.shape
    panel_rows, inner = w_key.shape
    heads = bias_table.shape[1]
    head_size = inner // heads
    rows = batch * heads
    me = lax.axis_index("mp").astype(jnp.int32)
    index = me.reshape(1)
    aligned = panel_rows % LANES == 0
    one_shot = aligned and mp <= ONE_SHOT and mp & (mp - 1) == 0
    slots = jnp.arange(mp, dtype=jnp.int32)
    copies = mp if one_shot else 1

    def sum_ready(value):
        if one_shot:
            return lax.all_to_all(value, "mp", 0, 0, tiled=True)
        return all_sum(value, "mp", mp)

    def swap(value, stride):
        return exchange(value, "mp", mp, stride)

    cols, gain = hidden, norm_gain.reshape(1, width)
    if not aligned:
        cols = lax.dynamic_slice_in_dim(cols, me * panel_rows, panel_rows, 1)
        gain = lax.dynamic_slice_in_dim(gain, me * panel_rows, panel_rows, 1)
    summand = jax.ShapeDtypeStruct((copies, batch, inner), F32)
    query = sum_ready(call(query_kernel, summand, 1, 4)(index, hidden, cols, gain, w_query))
    keyed = call(
        functools.partial(key_kernel, heads), jax.ShapeDtypeStruct((panel_rows, rows), BF16), 0, 2
    )(query, w_key)[None]

    enc_rows = enc_states.reshape(batch * src_local, width)
    span = min(rows, panel_rows)
    attend_outs = [
        jax.ShapeDtypeStruct((rows, batch * src_local), BF16),
        jax.ShapeDtypeStruct((EXTRA_ROWS, span), BF16),
    ]

    def piece_shape(count):
        return jax.ShapeDtypeStruct((count, rows + EXTRA_ROWS, panel_rows), BF16)

    def attend(pieces, layout, ids, out_layout, out_ids, part):
        arrays = [enc_rows, bias_table, buckets, *pieces] + part
        kernel = functools.partial(
            attend_kernel, layout, out_layout, panel_rows, heads,
            float(head_size) ** (-0.5), len(part) > 0,
        )
        outs = attend_outs + [piece_shape(count) for count in out_layout]
        return call(kernel, outs, 4, len(arrays), 24)(index, ids, out_ids, src_len, *arrays)

    if one_shot:
        strides = list(range(mp - 2, 0, -2))
        arrived = {0: keyed}
        for k in strides:
            arrived[k] = swap(keyed, k)
        for k in [0] + strides[::-1]:
            arrived[k + 1] = swap(arrived[k], 1)
        half = mp // 2
        early, late = list(range(half)), list(range(half, mp))
        ones = (1,) * half
        me_ids = slots ^ me
        part = call(
            functools.partial(score_kernel, ones),
            jax.ShapeDtypeStruct((batch * src_local, rows), F32), 1, 1 + half, 16,
        )(me_ids[:half], enc_rows, *[arrived[k] for k in early])
        targets = strides + [0]
        own_ids = jnp.array(targets, dtype=jnp.int32) ^ me
        turned, extra, *far = attend(
            [arrived[k] for k in late], ones, me_ids[half:], ones, own_ids ^ 1, [part]
        )
        far = [swap(piece, 1) for piece in far]
        near = call(
            functools.partial(mix_kernel, ones), [piece_shape(1)] * half, 1, 3, 16
        )(own_ids, enc_rows, turned, extra)
        pieces = [near[-1], far[-1]]
        for k, left, right in zip(strides, near, far):
            merged = call(merge_kernel, piece_shape(1), 0, 2)(left, right)
            pieces.append(swap(merged, k))
        layout = (1,) * len(pieces)
    else:
        layout = (mp,)
        gathered = lax.all_gather(keyed[0], "mp", axis=0)
        _, _, mixed = attend([gathered], layout, slots, layout, slots, [])
        pieces = [lax.all_to_all(mixed, "mp", 0, 0, tiled=True)]

    context = sum_ready(
        call(functools.partial(value_kernel, layout, heads), summand, 0, 1 + len(pieces))(
            w_value, *pieces
        )
    )
    out_cols = w_out.shape[1]
    partial = call(out_kernel, jax.ShapeDtypeStruct((batch, out_cols), F32), 0, 2)(context, w_out)
    summed = head_sum(partial, "head", head)
    residual = lax.dynamic_slice_in_dim(hidden, me * out_cols, out_cols, 1)
    return (summed + residual.astype(F32)).astype(BF16)


def solution(mesh):
    return jax.shard_map(
        functools.partial(shards, mesh.shape["mp"], mesh.shape["head"]),
        mesh=mesh,
        in_specs=(
            P(),
            P(),
            P("mp", "head"),
            P(None, "mp", None),
            P("mp", "head"),
            P("mp", "head"),
            P("head", "mp"),
            P(None, "head"),
            P(None, "mp"),
            P(),
        ),
        out_specs=P(None, "mp"),
        check_vma=False,
    )
```

```python
import functools

import jax
import jax.numpy as jnp
from jax import lax
from jax.experimental import pallas as pl
from jax.experimental.pallas import tpu as pltpu
from jax.sharding import PartitionSpec as P

EPSILON = 1e-06
NEGATIVE = -1e30
ONE_SHOT = 8
EXTRA_ROWS = 16
LANES = 128


VMEM = pl.BlockSpec(memory_space=pltpu.VMEM)
SMEM = pl.BlockSpec(memory_space=pltpu.SMEM)
HBM = pl.BlockSpec(memory_space=pltpu.HBM)
F32 = jnp.float32
BF16 = jnp.bfloat16


def exchange(value, axis, size, stride):
    return lax.ppermute(value, axis, [(i, i ^ stride) for i in range(size)])


def all_sum(value, axis, size):
    if size & (size - 1):
        return lax.psum(value, axis)
    stride = 1
    while stride < size:
        value = value + exchange(value, axis, size, stride)
        stride *= 2
    return value


def head_parts(value, axis, size):
    if size & (size - 1) or size > ONE_SHOT:
        return [all_sum(value, axis, size)]
    return [value] + [exchange(value, axis, size, k) for k in range(1, size)]


def dot(left, right, contract=((1,), (0,)), **kwargs):
    return lax.dot_general(left, right, (contract, ((), ())), preferred_element_type=F32, **kwargs)


def query_kernel(
    index_ref, hidden_hbm, cols_hbm, gain_hbm, wq_hbm, out_ref,
    hidden_ref, cols_ref, gain_ref, wq_ref, sems,
):
    panel_rows = wq_ref.shape[0]
    sources = [hidden_hbm, cols_hbm, gain_hbm, wq_hbm]
    targets = [hidden_ref, cols_ref, gain_ref, wq_ref]
    if cols_hbm.shape[1] != panel_rows:
        window = pl.ds(pl.multiple_of(index_ref[0] * panel_rows, panel_rows), panel_rows)
        sources[1:3] = [cols_hbm.at[:, window], gain_hbm.at[:, window]]
    copies = [
        pltpu.make_async_copy(source, target, sems.at[i])
        for i, (source, target) in enumerate(zip(sources, targets))
    ]
    for copy in copies:
        copy.start()
    for copy in copies[:3]:
        copy.wait()
    widened = hidden_ref[...].astype(F32)
    mean_square = jnp.mean(widened * widened, axis=-1, keepdims=True)
    own = cols_ref[...].astype(F32) * lax.rsqrt(mean_square + EPSILON) * gain_ref[...]
    copies[3].wait()
    out_ref[...] = dot(own.astype(BF16), wq_ref[...])


def load_kernel(source_ref, out_ref, sem):
    copy = pltpu.make_async_copy(source_ref, out_ref, sem)
    copy.start()
    copy.wait()


def total_of(refs):
    total = refs[0][...]
    for ref in refs[1:]:
        total = total + ref[...]
    return total


def key_kernel(heads, wk_ref, *refs):
    query_refs, out_ref = refs[:-1], refs[-1]
    batch, inner = query_refs[0].shape
    head_size = inner // heads
    rows = batch * heads
    query = total_of(query_refs).astype(BF16)
    column = lax.broadcasted_iota(jnp.int32, (batch, rows), 1) // heads
    column = (column == lax.broadcasted_iota(jnp.int32, (batch, rows), 0)).astype(BF16)
    blocks = dot(query, column, ((0,), (0,)))
    own_head = lax.broadcasted_iota(jnp.int32, (inner, rows), 0) // head_size
    row_head = lax.broadcasted_iota(jnp.int32, (inner, rows), 1) % heads
    blocks = jnp.where(own_head == row_head, blocks, 0.0).astype(BF16)
    out_ref[...] = dot(wk_ref[...], blocks).astype(BF16)


def window(offsets, index_ref, slot, panel_rows):
    if offsets is None:
        return slice(slot * panel_rows, (slot + 1) * panel_rows)
    owner = jnp.bitwise_xor(index_ref[0], offsets[slot])
    return pl.ds(pl.multiple_of(owner * panel_rows, panel_rows), panel_rows)


def slots_of(refs):
    return [(ref, i) for ref in refs for i in range(ref.shape[0])]


def score_sum(offsets, index_ref, enc_ref, refs):
    scores = None
    for slot, (ref, i) in enumerate(slots_of(refs)):
        term = dot(enc_ref[:, window(offsets, index_ref, slot, ref.shape[1])], ref[i])
        scores = term if scores is None else scores + term
    return scores


def score_kernel(offsets, heads, factor, index_ref, len_ref, enc_ref, table_ref, buckets_ref, *refs):
    scores = score_sum(offsets, index_ref, enc_ref, refs[:-1]) * factor
    batch, src_local = buckets_ref.shape
    kinds = table_ref.shape[1]
    rows = batch * heads
    table = jnp.concatenate([table_ref[...]] * batch, axis=0)
    kind_ids = lax.broadcasted_iota(jnp.int32, (kinds, src_local), 0)
    position = index_ref[0] * src_local + lax.broadcasted_iota(jnp.int32, (src_local, rows), 0)
    row_batch = lax.broadcasted_iota(jnp.int32, (src_local, rows), 1) // heads
    for b in range(batch):
        bias = dot(
            (buckets_ref[b : b + 1, :] == kind_ids).astype(F32),
            table,
            ((0,), (1,)),
            precision=lax.Precision.HIGHEST,
        )
        is_live = (position < len_ref[b]) & (row_batch == b)
        part = slice(b * src_local, (b + 1) * src_local)
        refs[-1][part, :] = jnp.where(is_live, scores[part, :] + bias, NEGATIVE)


def mix_pieces(offsets, index_ref, enc_ref, turned, extra, refs):
    rows, span = turned.shape[0], extra.shape[1]
    for slot, (ref, i) in enumerate(slots_of(refs)):
        panel_rows = ref.shape[2]
        ref[i, :rows, :] = dot(
            turned, enc_ref[:, window(offsets, index_ref, slot, panel_rows)]
        ).astype(BF16)
        if span != panel_rows:
            ref[i, rows:, :] = jnp.zeros((EXTRA_ROWS, panel_rows), BF16)
        ref[i, rows:, :span] = extra


def attend_kernel(offsets, out_offsets, factor, index_ref, enc_ref, part_ref, *refs):
    count = len(offsets) if offsets else 0
    piece_refs, turned_ref, extra_ref, out_refs = (
        refs[:count], refs[count], refs[count + 1], refs[count + 2 :],
    )
    scores = part_ref[...]
    is_live = scores > 0.5 * NEGATIVE
    if count:
        scores = scores + factor * score_sum(offsets, index_ref, enc_ref, piece_refs)
    shift = jnp.max(scores, axis=0, keepdims=True)
    shift = shift.astype(BF16).astype(F32)
    weights = jnp.where(is_live, jnp.exp(scores - shift), 0.0).astype(BF16).astype(F32)
    total = jnp.sum(weights, axis=0, keepdims=True)
    extra = extra_lines(shift, total, extra_ref.shape[1])
    extra_ref[...] = extra
    turned = weights.T.astype(BF16)
    turned_ref[...] = turned
    mix_pieces(out_offsets, index_ref, enc_ref, turned, extra, out_refs)


def mix_kernel(offsets, index_ref, enc_ref, turned_ref, extra_ref, *refs):
    mix_pieces(offsets, index_ref, enc_ref, turned_ref[...], extra_ref[...], refs)


def extra_lines(shift, total, span):
    high = total.astype(BF16).astype(F32)
    lines = [
        scalar[:, start : start + span]
        for scalar in (shift, high, total - high)
        for start in range(0, shift.shape[1], span)
    ]
    lines.append(jnp.zeros((EXTRA_ROWS - len(lines), span), F32))
    return jnp.concatenate(lines, axis=0).astype(BF16)


def read_extra(slots, rows, span):
    count = rows // span

    def scalar(extra, which):
        lines = [extra[which * count + j : which * count + j + 1] for j in range(count)]
        return jnp.concatenate(lines, axis=1)

    extras = [ref[i, rows:, :span].astype(F32) for ref, i in slots]
    shifts = jnp.concatenate([scalar(extra, 0) for extra in extras], axis=0)
    totals = jnp.concatenate([scalar(extra, 1) + scalar(extra, 2) for extra in extras], axis=0)
    return shifts, totals


def mix_sum(slots, scale, rows):
    scale = scale.T
    mixed = None
    for slot, (ref, i) in enumerate(slots):
        term = scale[:, slot : slot + 1] * ref[i, :rows, :].astype(F32)
        mixed = term if mixed is None else mixed + term
    return mixed


def merge_kernel(left_ref, right_ref, out_ref):
    rows, panel_rows = out_ref.shape[1] - EXTRA_ROWS, out_ref.shape[2]
    span = min(rows, panel_rows)
    slots = [(left_ref, 0), (right_ref, 0)]
    shifts, totals = read_extra(slots, rows, span)
    shift = jnp.max(shifts, axis=0, keepdims=True)
    scale = jnp.exp(shifts - shift)
    total = jnp.sum(scale * totals, axis=0, keepdims=True)
    out_ref[0, :rows, :] = mix_sum(slots, scale, rows).astype(BF16)
    if span != panel_rows:
        out_ref[0, rows:, :] = jnp.zeros((EXTRA_ROWS, panel_rows), BF16)
    out_ref[0, rows:, :span] = extra_lines(shift, total, span)


def value_kernel(heads, wv_ref, *refs):
    piece_refs, out_ref = refs[:-1], refs[-1]
    panel_rows, inner = wv_ref.shape
    rows = piece_refs[0].shape[1] - EXTRA_ROWS
    batch = rows // heads
    slots = slots_of(piece_refs)
    shifts, totals = read_extra(slots, rows, min(rows, panel_rows))
    scale = jnp.exp(shifts - jnp.max(shifts, axis=0, keepdims=True))
    scale = scale / jnp.sum(scale * totals, axis=0, keepdims=True)
    mixed = mix_sum(slots, scale, rows)
    high = mixed.astype(BF16)
    low = (mixed - high.astype(F32)).astype(BF16)
    product = dot(high, wv_ref[...]) + dot(low, wv_ref[...])
    row_head = lax.broadcasted_iota(jnp.int32, (rows, inner), 0) % heads
    own_head = lax.broadcasted_iota(jnp.int32, (rows, inner), 1) // (inner // heads)
    product = jnp.where(row_head == own_head, product, 0.0)
    out_ref[...] = jnp.sum(product.reshape(batch, heads, inner), axis=1)


def out_kernel(wo_ref, *refs):
    refs[-1][...] = dot(total_of(refs[:-1]).astype(BF16), wo_ref[...])


def final_kernel(index_ref, hidden_ref, *refs):
    out_ref = refs[-1]
    out_cols = out_ref.shape[1]
    own = pl.ds(pl.multiple_of(index_ref[0] * out_cols, out_cols), out_cols)
    out_ref[...] = (total_of(refs[:-1]) + hidden_ref[:, own].astype(F32)).astype(BF16)


def call(kernel, outs, scalars, arrays, limit=8):
    return pl.pallas_call(
        kernel,
        out_shape=outs,
        in_specs=[SMEM] * scalars + [VMEM] * arrays,
        compiler_params=pltpu.CompilerParams(vmem_limit_bytes=limit << 20),
    )


def on_chip(array):
    return pl.pallas_call(
        load_kernel,
        out_shape=jax.ShapeDtypeStruct(array.shape, array.dtype),
        in_specs=[HBM],
        out_specs=VMEM,
        scratch_shapes=[pltpu.SemaphoreType.DMA],
        compiler_params=pltpu.CompilerParams(vmem_limit_bytes=1 << 20),
    )(array)


def shards(
    mp, head,
    hidden, norm_gain, w_query, enc_states, w_key, w_value, w_out, bias_table, buckets, src_len,
):
    batch, src_local, width = enc_states.shape
    panel_rows, inner = w_key.shape
    heads = bias_table.shape[1]
    head_size = inner // heads
    rows = batch * heads
    me = lax.axis_index("mp").astype(jnp.int32)
    index = me.reshape(1)
    aligned = panel_rows % LANES == 0
    one_shot = aligned and mp <= ONE_SHOT and mp & (mp - 1) == 0

    def swap(value, stride):
        return exchange(value, "mp", mp, stride)

    def sum_parts(value):
        if not one_shot:
            return [all_sum(value, "mp", mp)]
        parts = [value] + [swap(value, k) for k in range(1, min(mp, 4))]
        stride = len(parts)
        while stride < mp:
            value = sum(parts[1:], parts[0])
            parts = [value, swap(value, stride)]
            stride *= 2
        return parts

    enc_rows = on_chip(enc_states.reshape(batch * src_local, width))
    w_key = on_chip(w_key)
    cols, gain = hidden, norm_gain.reshape(1, width)
    if not aligned:
        cols = lax.dynamic_slice_in_dim(cols, me * panel_rows, panel_rows, 1)
        gain = lax.dynamic_slice_in_dim(gain, me * panel_rows, panel_rows, 1)
    summand = jax.ShapeDtypeStruct((batch, inner), F32)
    query = pl.pallas_call(
        query_kernel,
        out_shape=summand,
        in_specs=[SMEM] + [HBM] * 4,
        scratch_shapes=[
            pltpu.VMEM((batch, width), BF16),
            pltpu.VMEM((batch, panel_rows), BF16),
            pltpu.VMEM((1, panel_rows), F32),
            pltpu.VMEM((panel_rows, inner), BF16),
            pltpu.SemaphoreType.DMA((4,)),
        ],
        compiler_params=pltpu.CompilerParams(vmem_limit_bytes=59 << 20),
    )(index, hidden, cols, gain, w_query)
    query = sum_parts(query)
    keyed = call(
        functools.partial(key_kernel, heads),
        jax.ShapeDtypeStruct((panel_rows, rows), BF16), 0, 1 + len(query),
    )(w_key, *query)[None]

    span = min(rows, panel_rows)
    factor = float(head_size) ** (-0.5)

    def piece_shape(count):
        return jax.ShapeDtypeStruct((count, rows + EXTRA_ROWS, panel_rows), BF16)

    def score(pieces, offsets):
        arrays = [enc_rows, bias_table.T, buckets, *pieces]
        return call(
            functools.partial(score_kernel, offsets, heads, factor),
            jax.ShapeDtypeStruct((batch * src_local, rows), F32), 2, len(arrays), 12,
        )(index, src_len, *arrays)

    def attend(part, pieces, offsets, out_counts, out_offsets):
        arrays = [enc_rows, part, *pieces]
        outs = [
            jax.ShapeDtypeStruct((rows, batch * src_local), BF16),
            jax.ShapeDtypeStruct((EXTRA_ROWS, span), BF16),
        ] + [piece_shape(count) for count in out_counts]
        return call(
            functools.partial(attend_kernel, offsets, out_offsets, factor), outs, 1, len(arrays), 12
        )(index, *arrays)

    if one_shot:
        strides = list(range(mp - 2, 0, -2))
        half = mp // 2
        arrived = {0: keyed}
        for k in strides:
            arrived[k] = swap(keyed, k)
        for k in [0] + strides[::-1]:
            arrived[k + 1] = swap(arrived[k], 1)
        part = score([arrived[k] for k in range(half)], tuple(range(half)))
        targets = tuple(strides) + (0,)
        turned, extra, *far = attend(
            part,
            [arrived[k] for k in range(half, mp)],
            tuple(range(half, mp)),
            (1,) * half,
            tuple(k ^ 1 for k in targets),
        )
        far = [swap(piece, 1) for piece in far]
        near = call(
            functools.partial(mix_kernel, targets), [piece_shape(1)] * half, 1, 3, 12
        )(index, enc_rows, turned, extra)
        pieces = [near[-1], far[-1]]
        for k, left, right in zip(strides, near, far):
            merged = call(merge_kernel, piece_shape(1), 0, 2)(left, right)
            pieces.append(swap(merged, k))
    else:
        part = score([lax.all_gather(keyed[0], "mp", axis=0)], None)
        _, _, mixed = attend(part, [], None, (mp,), None)
        pieces = [lax.all_to_all(mixed, "mp", 0, 0, tiled=True)]

    context = sum_parts(
        call(functools.partial(value_kernel, heads), summand, 0, 1 + len(pieces))(w_value, *pieces)
    )
    out_cols = w_out.shape[1]
    partial = call(
        out_kernel, jax.ShapeDtypeStruct((batch, out_cols), F32), 0, 1 + len(context)
    )(w_out, *context)
    parts = head_parts(partial, "head", head)
    if out_cols % LANES:
        residual = lax.dynamic_slice_in_dim(hidden, me * out_cols, out_cols, 1)
        return (sum(parts) + residual.astype(F32)).astype(BF16)
    return call(
        final_kernel, jax.ShapeDtypeStruct((batch, out_cols), BF16), 1, 1 + len(parts)
    )(index, hidden, *parts)


def solution(mesh):
    return jax.shard_map(
        functools.partial(shards, mesh.shape["mp"], mesh.shape["head"]),
        mesh=mesh,
        in_specs=(
            P(),
            P(),
            P("mp", "head"),
            P(None, "mp", None),
            P("mp", "head"),
            P("mp", "head"),
            P("head", "mp"),
            P(None, "head"),
            P(None, "mp"),
            P(),
        ),
        out_specs=P(None, "mp"),
        check_vma=False,
    )
```
